32 devices in a mesh: row: 4 (over z), col: 8 (over y, x, core).
Axes of the slice: x: 2, y: 2, z: 4, core: 2. Of those that a mesh axis runs over, the one named last changes fastest.
Arguments:
- tokens: bfloat16 [2048, 8192], P('row', 'col'), may hold values from -6 to 6
- weight: bfloat16 [8192, 26624], P('row', 'col'), may hold values from -0.0625 to 0.0625
- out_grad: bfloat16 [2048, 26624], P('row', 'col'), may hold values from -6 to 6
Outputs:
- preact: bfloat16 [2048, 26624], P('row', 'col')
- input_grad: bfloat16 [2048, 8192], P('row', 'col')
The draws below stay inside these ranges and needn't reach their ends.
All inputs are finite; a program needn't handle non-finite values.
Results may differ from the reference program's by a relative error of at most 0.0049.
Values may be sent and summed in bfloat16 or wider, within the bound.
A program may use at most 192 MiB of HBM per device.

```python
import math
import jax
import jax.numpy as jnp

D = 8192
FF = 26624
TOKENS = 2048


def block_scale(rng, dims, shards, low, largest):
    gain = 1.0
    for dim, blocks in shards:
        steps = jax.random.uniform(jax.random.fold_in(jax.random.fold_in(rng, 6), dim), (blocks,), jnp.float32, low / len(shards), largest / len(shards))
        gain = gain * jnp.repeat(jnp.exp(steps), dims[dim] // blocks).reshape((-1,) + (1,) * (len(dims) - 1 - dim))
    return gain


def scatter_about(stream_key, dims, spread, most, pieces=(), held_as=jnp.bfloat16):
    factor_of = block_scale(stream_key, dims, pieces, -0.22, 0.18) if pieces else 1.0
    drawn = jax.random.normal(stream_key, dims, jnp.float32) * spread * factor_of
    return jnp.minimum(jnp.maximum(drawn, -most), most).astype(held_as)


def setup_inputs(seed: int = 0) -> dict:
    streams_of = jax.random.split(jax.random.key(seed), 4)
    tokens = scatter_about(streams_of[0], (TOKENS, D), 1.0, 6.0, ((0, 4), (1, 8)))
    weight = scatter_about(streams_of[1], (D, FF), D ** -0.5, 0.0625, ((0, 4), (1, 8)))
    out_grad = scatter_about(streams_of[2], (TOKENS, FF), 1.0, 6.0, ((0, 4), (1, 8)))
    return dict(tokens=tokens, weight=weight, out_grad=out_grad)


sqrt_half = 1.0 / math.sqrt(2.0)
inv_root_tau = 1.0 / math.sqrt(2.0 * math.pi)

def gelu_slope(values):
    return 0.5 * (1.0 + jax.scipy.special.erf(values * sqrt_half)) + values * jnp.exp(-0.5 * values * values) * inv_root_tau

def reference(tokens, weight, out_grad):
    full_pre = jnp.dot(tokens, weight, preferred_element_type=jnp.float32)
    preact = full_pre.astype(jnp.bfloat16)
    gradient = (out_grad.astype(jnp.float32) * gelu_slope(full_pre)).astype(jnp.bfloat16)
    input_grad = jnp.dot(gradient, weight.T, preferred_element_type=jnp.float32).astype(jnp.bfloat16)
    return (preact, input_grad)
```

```python
import functools
import math

import jax
import jax.numpy as jnp
from jax import lax
from jax.experimental import pallas as pl
from jax.experimental.pallas import tpu as pltpu
from jax.sharding import PartitionSpec as P

sqrt_half = 1.0 / math.sqrt(2.0)
inv_root_tau = 1.0 / math.sqrt(2.0 * math.pi)

MESH = pl.DeviceIdType.MESH
CHUNKS = 4
WIDTH = 256
LAG = 1
OUT_SLOTS = 3


def gelu_slope(values):
    return (
        0.5 * (1.0 + lax.erf(values * sqrt_half))
        + values * jnp.exp(-0.5 * values * values) * inv_root_tau
    )


class Plan:
    def __init__(self, rows, cols, tokens, weight):
        self.rows, self.cols = rows, cols
        self.count, self.share = tokens.shape
        self.features, self.hidden = weight.shape
        self.ratio = self.features // self.share
        self.chips = cols // 2
        self.chunks = CHUNKS
        self.size = self.count // CHUNKS
        self.piece = self.size // cols
        self.width = WIDTH
        self.slices = self.hidden // WIDTH
        self.units = self.chunks * self.slices
        self.far = rows - 1
        self.slope_lag = self.far * LAG
        self.down_lag = 2 * self.far * LAG
        self.hold = self.slope_lag + 1
        self.in_slots = rows * LAG + 2
        self.grad_slots = rows * LAG + 3

    def scratch(self):
        bf, f4 = jnp.bfloat16, jnp.float32
        r, c, n, s, d = self.rows, self.cols, self.chunks, self.size, self.features
        far, w, piece, chips = self.far, self.width, self.piece, self.chips
        dma = pltpu.SemaphoreType.DMA
        return dict(
            a1=pltpu.VMEM((n, r, piece, d), bf),
            a2=pltpu.VMEM((n, r, piece, d), bf),
            tok=pltpu.VMEM((n, r, c, piece, d), bf),
            wv=pltpu.VMEM((self.slices, d, w), bf),
            part=pltpu.VMEM((self.hold, r * s, w), f4),
            rin=pltpu.VMEM((self.in_slots, 2, far, s, w), bf),
            rout=pltpu.VMEM((OUT_SLOTS, 2, far, s, w), bf),
            grad=pltpu.VMEM((self.grad_slots, r, s, w), bf),
            og=pltpu.VMEM((2, s, w), bf),
            pre=pltpu.VMEM((2, s, w), bf),
            acc=pltpu.VMEM((2, r, c, piece, d), f4),
            x_out=pltpu.VMEM((chips, r, piece, d), bf),
            x_in=pltpu.VMEM((2, chips, r, piece, d), bf),
            y_out=pltpu.VMEM((chips, r, piece, d), bf),
            y_in=pltpu.VMEM((2, chips, r, piece, d), bf),
            t_out=pltpu.VMEM((r, piece, d), bf),
            t_in=pltpu.VMEM((2, r, piece, d), bf),
            w_sem=dma((self.slices,)),
            s1s=dma((n, c)),
            s1r=dma((n, c)),
            s2s=dma((n, r)),
            s2r=dma((n, r)),
            s3s=dma((n, chips + 1)),
            s3r=dma((n, chips + 1)),
            s4s=dma((n, chips)),
            s4r=dma((n, chips)),
            rss=dma((OUT_SLOTS, 2, far)),
            rsr=dma((self.in_slots, 2, far)),
            ags=dma((self.grad_slots, 2, far)),
            agr=dma((self.grad_slots, 2, far)),
            og_sem=dma((2,)),
            pre_sem=dma((2,)),
            d1s=dma((chips,)),
            d1r=dma((2, chips)),
            d2s=dma((chips,)),
            d2r=dma((2, chips)),
            d3s=dma((r,)),
            d3r=dma((2, r)),
            d4s=dma((c,)),
            d4r=dma((n, c)),
        )


def aligned(index, size):
    return pl.ds(pl.multiple_of(index * size, size), size)


def body(pn, names, tokens, weight, out_grad, preact, input_grad, *refs):
    b = dict(zip(names, refs))
    rows, cols, chips, far = pn.rows, pn.cols, pn.chips, pn.far
    size, piece, width, share = pn.size, pn.piece, pn.width, pn.share
    units, slices, ratio = pn.units, pn.slices, pn.ratio
    r, c = lax.axis_index("row"), lax.axis_index("col")
    core, chip = c % 2, c // 2
    partner = c + 1 - 2 * core

    def remote(src, dst, send, recv, to):
        return pltpu.make_async_remote_copy(
            src_ref=src, dst_ref=dst, send_sem=send, recv_sem=recv, device_id=to, device_id_type=MESH
        )

    barrier = pltpu.get_barrier_semaphore()
    for j in range(1, rows):
        pl.semaphore_signal(barrier, inc=1, device_id=((r + j) % rows, c), device_id_type=MESH)
    for j in range(1, cols):
        pl.semaphore_signal(barrier, inc=1, device_id=(r, (c + j) % cols), device_id_type=MESH)
    pl.semaphore_wait(barrier, rows + cols - 2)

    def spread(k, j):
        to = (c + j) % cols
        src = tokens.at[aligned(k * cols + to, piece), :]
        dst = b["a1"].at[k, c // ratio, :, aligned(c % ratio, share)]
        if not j:
            return pltpu.make_async_copy(src, dst, b["s1s"].at[k, 0])
        return remote(src, dst, b["s1s"].at[k, j], b["s1r"].at[k, j], (r, to))

    def exchange(k, j):
        to = (r + j) % rows
        src, dst = b["a1"].at[k, to], b["a2"].at[k, r]
        if not j:
            return pltpu.make_async_copy(src, dst, b["s2s"].at[k, 0])
        return remote(src, dst, b["s2s"].at[k, j], b["s2r"].at[k, j], (to, c))

    def gather(k, j):
        src, dst = b["a2"].at[k], b["tok"].at[k, :, c]
        if not j:
            return pltpu.make_async_copy(src, dst, b["s3s"].at[k, 0])
        to = partner if j == chips else ((chip + j) % chips) * 2 + core
        return remote(src, dst, b["s3s"].at[k, j], b["s3r"].at[k, j], (r, to))

    def pass_on(k, j):
        here = b["tok"].at[k, :, ((chip - j + chips) % chips) * 2 + core]
        return remote(here, here, b["s4s"].at[k, j], b["s4r"].at[k, j], (r, partner))

    def begin(copy, k, number):
        for j in range(1, number):
            copy(k, j).start()
        copy(k, 0).start()

    def finish(copy, k, number):
        copy(k, 0).wait()
        for j in range(1, number):
            copy(k, j).wait_recv()
        for j in range(1, number):
            copy(k, j).wait_send()

    def stage1(k):
        begin(spread, k, cols)

    def stage2(k):
        finish(spread, k, cols)
        begin(exchange, k, rows)

    def stage3(k):
        finish(exchange, k, rows)
        begin(gather, k, chips + 1)

    def stage4(k):
        for j in range(1, chips):
            gather(k, j).wait_recv()
            pass_on(k, j).start()

    def stage5(k):
        gather(k, 0).wait()
        gather(k, chips).wait_recv()
        for j in range(1, chips + 1):
            gather(k, j).wait_send()
        for j in range(1, chips):
            pass_on(k, j).wait()

    def w_copy(g):
        return pltpu.make_async_copy(
            weight.at[:, aligned(g, width)], b["wv"].at[g], b["w_sem"].at[g]
        )

    stage1(0)

    @pl.loop(0, slices)
    def _(g):
        w_copy(g).start()

    stage2(0)
    stage3(0)
    stage4(0)

    def place(v):
        return aligned(v // slices, size), aligned(v % slices, width)

    def up(v):
        k, g = v // slices, v % slices

        @pl.when(g == 0)
        def _():
            stage5(k)

        @pl.when(k == 0)
        def _():
            w_copy(g).wait()

        b["part"][v % pn.hold] = jnp.dot(
            b["tok"][k].reshape(rows * size, pn.features),
            b["wv"][g],
            preferred_element_type=jnp.float32,
        )

    def towards(way):
        return r if way == 0 else far - r

    def sum_copy(v, way, h):
        slot = v % OUT_SLOTS
        return remote(
            b["rout"].at[slot, way, h],
            b["rin"].at[v % pn.in_slots, way, h],
            b["rss"].at[slot, way, h],
            b["rsr"].at[v % pn.in_slots, way, h],
            ((r + 1) % rows if way == 0 else (r + far) % rows, c),
        )

    def sums(v, h):
        for way in (0, 1):
            pos = towards(way)

            @pl.when(pos <= h)
            def _(way=way, pos=pos):
                @pl.when(v >= OUT_SLOTS)
                def _():
                    sum_copy(v, way, h).wait_send()

                owner = pos + far - h
                owner = owner if way == 0 else far - owner
                mine = b["part"].at[v % pn.hold, aligned(owner, size), :]
                out = b["rout"].at[v % OUT_SLOTS, way, h]

                @pl.when(pos == 0)
                def _():
                    out[...] = mine[...].astype(jnp.bfloat16)

                if h:

                    @pl.when(pos > 0)
                    def _():
                        sum_copy(v, way, h - 1).wait_recv()
                        got = b["rin"][v % pn.in_slots, way, h - 1]
                        out[...] = (got.astype(jnp.float32) + mine[...]).astype(jnp.bfloat16)

                sum_copy(v, way, h).start()

    def og_copy(v):
        return pltpu.make_async_copy(out_grad.at[place(v)], b["og"].at[v % 2], b["og_sem"].at[v % 2])

    def pre_copy(v):
        return pltpu.make_async_copy(b["pre"].at[v % 2], preact.at[place(v)], b["pre_sem"].at[v % 2])

    def grad_copy(v, way, h):
        slot = v % pn.grad_slots
        source = lax.rem(r + (rows - h if way == 0 else h), rows)
        block = b["grad"].at[slot, source]
        return remote(
            block,
            block,
            b["ags"].at[slot, way, h],
            b["agr"].at[slot, way, h],
            ((r + 1) % rows if way == 0 else (r + far) % rows, c),
        )

    def slope(v):
        mine = b["part"].at[v % pn.hold, aligned(r, size), :]
        for way in (0, 1):

            @pl.when(towards(way) > 0)
            def _(way=way):
                sum_copy(v, way, far - 1).wait_recv()
                mine[...] += b["rin"][v % pn.in_slots, way, far - 1].astype(jnp.float32)

        og_copy(v).wait()

        @pl.when(v >= 2)
        def _():
            pre_copy(v).wait()

        full_pre = mine[...]
        gradient = b["og"][v % 2].astype(jnp.float32) * gelu_slope(full_pre)
        b["grad"][v % pn.grad_slots, r] = gradient.astype(jnp.bfloat16)
        for way in (0, 1):

            @pl.when(towards(way) < far)
            def _(way=way):
                grad_copy(v, way, 0).start()

        b["pre"][v % 2] = full_pre.astype(jnp.bfloat16)
        pre_copy(v).start()

        @pl.when(v + 1 < units)
        def _():
            og_copy(v + 1).start()

    def grads(v, h):
        for way in (0, 1):

            @pl.when(towards(way) >= h)
            def _(way=way):
                grad_copy(v, way, h - 1).wait_recv()

                @pl.when(towards(way) < far)
                def _():
                    grad_copy(v, way, h).start()

    def down(v):
        k, g = v // slices, v % slices
        for way in (0, 1):

            @pl.when(towards(way) == far)
            def _(way=way):
                grad_copy(v, way, far - 1).wait_recv()

        acc = b["acc"].at[k % 2]

        @pl.when(g == 0)
        def _():
            acc[...] = jnp.zeros_like(acc)

        step = min(512, pn.features)
        blocks = b["grad"][v % pn.grad_slots].reshape(rows * size, width)
        for n in range(pn.features // step):
            part = lax.dot_general(
                blocks,
                b["wv"][g, n * step : (n + 1) * step],
                (((1,), (1,)), ((), ())),
                preferred_element_type=jnp.float32,
            )
            acc[:, :, :, n * step : (n + 1) * step] += part.reshape(rows, cols, piece, step)
        for way in (0, 1):
            for h in range(far):

                @pl.when((towards(way) >= h) & (towards(way) < far))
                def _(way=way, h=h):
                    grad_copy(v, way, h).wait_send()

    def pair_copy(k, q):
        return remote(
            b["x_out"].at[q], b["x_in"].at[k % 2, q], b["d1s"].at[q], b["d1r"].at[k % 2, q], (r, partner)
        )

    def plane_copy(k, j):
        to = ((chip + j) % chips) * 2 + core
        return remote(
            b["y_out"].at[j], b["y_in"].at[k % 2, j], b["d2s"].at[j], b["d2r"].at[k % 2, j], (r, to)
        )

    def row_copy(k, j):
        to = (r + j) % rows
        src, dst = b["t_out"].at[to], b["t_in"].at[k % 2, r]
        if not j:
            return pltpu.make_async_copy(src, dst, b["d3s"].at[0])
        return remote(src, dst, b["d3s"].at[j], b["d3r"].at[k % 2, j], (to, c))

    def owner_copy(k, j):
        to = (c + j) % cols
        src = b["t_in"].at[k % 2, to // ratio, :, aligned(to % ratio, share)]
        dst = input_grad.at[aligned(k * cols + c, piece), :]
        if not j:
            return pltpu.make_async_copy(src, dst, b["d4s"].at[0])
        return remote(src, dst, b["d4s"].at[j], b["d4r"].at[k, j], (r, to))

    def pair(k):
        for q in range(chips):

            @pl.when(k > 0)
            def _(q=q):
                pair_copy(k, q).wait_send()

            b["x_out"][q] = b["acc"][k % 2, :, q * 2 + 1 - core].astype(jnp.bfloat16)
            pair_copy(k, q).start()

    def plane(k):
        for q in range(chips):
            pair_copy(k, q).wait_recv()
        for j in list(range(1, chips)) + [0]:
            q = (chip + j) % chips
            total = b["acc"][k % 2, :, q * 2 + core] + b["x_in"][k % 2, q].astype(jnp.float32)
            if j:

                @pl.when(k > 0)
                def _(j=j):
                    plane_copy(k, j).wait_send()

                b["y_out"][j] = total.astype(jnp.bfloat16)
                plane_copy(k, j).start()
            else:
                b["acc"][k % 2, :, q * 2 + core] = total

    def owners_wait():
        for j in range(1, cols):
            owner_copy(0, j).wait_send()
        owner_copy(0, 0).wait()

    def exchange_back(k):
        @pl.when(k > 0)
        def _():
            owners_wait()
            for j in range(1, rows):
                row_copy(k, j).wait_send()

        total = b["acc"][k % 2, :, c]
        for j in range(1, chips):
            plane_copy(k, j).wait_recv()
            total = total + b["y_in"][k % 2, j].astype(jnp.float32)
        b["t_out"][...] = total.astype(jnp.bfloat16)
        for j in range(1, rows):
            row_copy(k, j).start()
        row_copy(k, 0).start()

    def owners(k):
        row_copy(k, 0).wait()
        for j in range(1, rows):
            row_copy(k, j).wait_recv()
        for j in range(1, cols):
            owner_copy(k, j).start()
        owner_copy(k, 0).start()

    def in_range(v):
        return (v >= 0) & (v < units)

    def at_chunk_end(v, action):
        @pl.when(in_range(v) & (v % slices == slices - 1))
        def _():
            action(v // slices)

    og_copy(0).start()
    ends = (0, 1, 3, 5)

    @pl.loop(0, units + pn.down_lag + ends[-1] + 1)
    def _(i):
        @pl.when(i < units)
        def _():
            up(i)

        for h in range(far):
            v = i - h * LAG

            @pl.when(in_range(v))
            def _(v=v, h=h):
                sums(v, h)

        @pl.when(in_range(i - pn.slope_lag))
        def _():
            slope(i - pn.slope_lag)

        for h in range(1, far):
            v = i - pn.slope_lag - h * LAG

            @pl.when(in_range(v))
            def _(v=v, h=h):
                grads(v, h)

        @pl.when(in_range(i - pn.down_lag))
        def _():
            down(i - pn.down_lag)

        for lag, action in zip(ends, (pair, plane, exchange_back, owners)):
            at_chunk_end(i - pn.down_lag - lag, action)

        for at, action in enumerate((stage1, stage2, stage3, stage4)):

            @pl.when((i < units - slices) & (i % slices == at * slices // 4))
            def _(action=action):
                action(i // slices + 1)

    for back in range(1, OUT_SLOTS + 1):
        for way in (0, 1):
            for h in range(far):

                @pl.when(towards(way) <= h)
                def _(back=back, way=way, h=h):
                    sum_copy(units - back, way, h).wait_send()

    for v in (units - 2, units - 1):
        pre_copy(v).wait()
    last = pn.chunks - 1
    for q in range(chips):
        pair_copy(last, q).wait_send()
    for j in range(1, chips):
        plane_copy(last, j).wait_send()
    for j in range(1, rows):
        row_copy(last, j).wait_send()
    owners_wait()

    @pl.loop(0, pn.chunks)
    def _(k):
        for j in range(1, cols):
            owner_copy(k, j).wait_recv()


def per_device(rows, cols, tokens, weight, out_grad):
    pn = Plan(rows, cols, tokens, weight)
    scratch = pn.scratch()
    anywhere = pl.BlockSpec(memory_space=pl.ANY)
    flops = 4 * pn.count * rows * pn.features * pn.hidden
    return pl.pallas_call(
        functools.partial(body, pn, tuple(scratch)),
        out_shape=(
            jax.ShapeDtypeStruct(out_grad.shape, jnp.bfloat16),
            jax.ShapeDtypeStruct(tokens.shape, jnp.bfloat16),
        ),
        in_specs=[anywhere] * 3,
        out_specs=(anywhere, anywhere),
        scratch_shapes=list(scratch.values()),
        compiler_params=pltpu.CompilerParams(
            collective_id=0, has_side_effects=True, vmem_limit_bytes=62 * 2**20
        ),
        cost_estimate=pl.CostEstimate(flops=flops, bytes_accessed=2 * weight.size, transcendentals=0),
    )(tokens, weight, out_grad)


def solution(mesh):
    rows, cols = mesh.shape["row"], mesh.shape["col"]
    return jax.shard_map(
        functools.partial(per_device, rows, cols),
        mesh=mesh,
        in_specs=(P("row", "col"), P("row", "col"), P("row", "col")),
        out_specs=(P("row", "col"), P("row", "col")),
        check_vma=False,
    )
```

```python
import functools
import math

import jax
import jax.numpy as jnp
from jax import lax
from jax.experimental import pallas as pl
from jax.experimental.pallas import tpu as pltpu
from jax.sharding import PartitionSpec as P

sqrt_half = 1.0 / math.sqrt(2.0)
inv_root_tau = 1.0 / math.sqrt(2.0 * math.pi)

MESH = pl.DeviceIdType.MESH
CHUNKS = 8
WIDTH = 256
LAG = 2
OUT_SLOTS = 3
AHEAD = 4


def gelu_slope(values):
    return (
        0.5 * (1.0 + lax.erf(values * sqrt_half))
        + values * jnp.exp(-0.5 * values * values) * inv_root_tau
    )


class Plan:
    def __init__(self, rows, cols, tokens, weight):
        self.rows, self.cols = rows, cols
        self.count, self.share = tokens.shape
        self.features, self.hidden = weight.shape
        self.ratio = self.features // self.share
        self.chips = cols // 2
        self.chunks = CHUNKS
        self.size = self.count // CHUNKS
        self.thin = max(self.share // cols, min(self.share, 128))
        self.across = self.share // self.thin
        self.deep = cols // self.across
        self.short = self.size // self.deep
        self.piece = self.ratio * self.thin
        self.width = WIDTH if self.hidden % WIDTH == 0 else 128
        self.slices = self.hidden // self.width
        assert self.deep * self.short * CHUNKS == self.count and self.slices * self.width == self.hidden
        self.units = self.chunks * self.slices
        self.far = rows - 1
        self.lag = LAG if rows <= 4 else 1
        self.ahead = min(AHEAD, self.chunks)
        self.slope_lag = self.far * self.lag
        self.down_lag = 2 * self.far * self.lag
        self.hold = self.slope_lag + 1
        self.in_slots = rows * self.lag + 2
        self.grad_slots = rows * self.lag + 3

    def scratch(self):
        bf, f4 = jnp.bfloat16, jnp.float32
        r, c, n, s, d = self.rows, self.cols, self.chunks, self.size, self.features
        far, w, piece, chips = self.far, self.width, self.piece, self.chips
        low = self.short
        dma = pltpu.SemaphoreType.DMA
        return dict(
            a1=pltpu.VMEM((n, r, low, piece), bf),
            a2=pltpu.VMEM((n, r, low, piece), bf),
            tok=pltpu.VMEM((n, r, s, d), bf),
            wv=pltpu.VMEM((self.slices, self.across, self.ratio, self.thin, w), bf),
            part=pltpu.VMEM((self.hold, r * s, w), f4),
            rin=pltpu.VMEM((self.in_slots, 2, far, s, w), bf),
            rout=pltpu.VMEM((OUT_SLOTS, 2, far, s, w), bf),
            grad=pltpu.VMEM((self.grad_slots, r, s, w), bf),
            og=pltpu.VMEM((2, s, w), bf),
            pre=pltpu.VMEM((2, s, w), bf),
            acc=pltpu.VMEM((2, self.across, r, s, piece), f4),
            x_out=pltpu.VMEM((chips, r, low, piece), bf),
            x_in=pltpu.VMEM((2, chips, r, low, piece), bf),
            y_out=pltpu.VMEM((chips, r, low, piece), bf),
            y_in=pltpu.VMEM((2, chips, r, low, piece), bf),
            t_out=pltpu.VMEM((r, low, piece), bf),
            t_in=pltpu.VMEM((2, r, low, piece), bf),
            w_sem=dma((self.slices, self.ratio)),
            s1s=dma((n, c)),
            s1r=dma((n, c)),
            s2s=dma((n, r)),
            s2r=dma((n, r)),
            s3s=dma((2, r, chips + 1)),
            s3r=dma((2, r, chips + 1)),
            s4s=dma((2, r, chips)),
            s4r=dma((2, r, chips)),
            rss=dma((OUT_SLOTS, 2, far)),
            rsr=dma((self.in_slots, 2, far)),
            ags=dma((self.grad_slots, 2, far)),
            agr=dma((self.grad_slots, 2, far)),
            og_sem=dma((2,)),
            pre_sem=dma((2,)),
            d1s=dma((chips,)),
            d1r=dma((2, chips)),
            d2s=dma((chips, r)),
            d2r=dma((2, chips, r)),
            d3s=dma((r,)),
            d3r=dma((2, r)),
            d4s=dma((c,)),
            d4r=dma((n, c)),
        )


def aligned(index, size):
    return pl.ds(pl.multiple_of(index * size, size), size)


def body(pn, names, tokens, weight, out_grad, preact, input_grad, *refs):
    b = dict(zip(names, refs))
    rows, cols, chips, far = pn.rows, pn.cols, pn.chips, pn.far
    size, piece, width, thin = pn.size, pn.piece, pn.width, pn.thin
    units, slices, ratio = pn.units, pn.slices, pn.ratio
    r, c = lax.axis_index("row"), lax.axis_index("col")
    core, chip = c % 2, c // 2
    partner = c + 1 - 2 * core
    across, deep, short = pn.across, pn.deep, pn.short

    def tall(q):
        return (q // across if deep > 1 else 0), (q % across if deep > 1 else q)


    def remote(src, dst, send, recv, to):
        return pltpu.make_async_remote_copy(
            src_ref=src, dst_ref=dst, send_sem=send, recv_sem=recv, device_id=to, device_id_type=MESH
        )

    barrier = pltpu.get_barrier_semaphore()
    for j in range(1, rows):
        pl.semaphore_signal(barrier, inc=1, device_id=((r + j) % rows, c), device_id_type=MESH)
    for j in range(1, cols):
        pl.semaphore_signal(barrier, inc=1, device_id=(r, (c + j) % cols), device_id_type=MESH)
    pl.semaphore_wait(barrier, rows + cols - 2)

    def others(action, far_first=False):
        steps = [s for d in range(1, rows) for s in (d, -d)]
        for s in steps[::-1] if far_first else steps:

            @pl.when((r + s >= 0) & (r + s < rows))
            def _(s=s):
                action(r + s)

    def spread(k, j):
        to = (c + j) % cols
        down_part, side = tall(to)
        src = tokens.at[aligned(k * deep + down_part, short), aligned(side, thin)]
        dst = b["a1"].at[k, c // ratio, :, aligned(c % ratio, thin)]
        if not j:
            return pltpu.make_async_copy(src, dst, b["s1s"].at[k, 0])
        return remote(src, dst, b["s1s"].at[k, j], b["s1r"].at[k, j], (r, to))

    def exchange(k, to):
        return remote(
            b["a1"].at[k, to], b["a2"].at[k, r], b["s2s"].at[k, to], b["s2r"].at[k, r], (to, c)
        )

    def exchanged(k, source):
        return remote(
            b["a1"].at[k, r], b["a2"].at[k, source], b["s2s"].at[k, r], b["s2r"].at[k, source], (source, c)
        )

    def token_part(k, row, q):
        down_part, side = tall(q)
        return b["tok"].at[k, row, aligned(down_part, short), aligned(side, piece)]

    def gather(k, row, j, own=False):
        src = b["a1"].at[k, r] if own else b["a2"].at[k, row]
        dst = token_part(k, row, c)
        send = b["s3s"].at[k % 2, row, j]
        if not j:
            return pltpu.make_async_copy(src, dst, send)
        to = partner if j == chips else ((chip + j) % chips) * 2 + core
        return remote(src, dst, send, b["s3r"].at[k % 2, row, j], (r, to))

    def pass_on(k, row, j):
        here = token_part(k, row, ((chip - j + chips) % chips) * 2 + core)
        return remote(here, here, b["s4s"].at[k % 2, row, j], b["s4r"].at[k % 2, row, j], (r, partner))

    def stage1(k):
        for j in range(1, cols):
            spread(k, j).start()
        spread(k, 0).start()

    def stage2(k):
        spread(k, 0).wait()
        for j in range(1, cols):
            spread(k, j).wait_recv()
        others(lambda to: exchange(k, to).start(), far_first=True)
        for j in range(1, cols):
            spread(k, j).wait_send()

    def gather_row(k, row, own=False):
        for j in list(range(1, chips + 1)) + [0]:
            gather(k, row, j, own).start()

    def stage3(k, with_own=True):
        if with_own:
            gather_row(k, r, own=True)

        def action(row):
            exchanged(k, row).wait_recv()
            gather_row(k, row)

        others(action)

    def stage4(k):
        def action(row):
            for j in range(1, chips):
                gather(k, row, j).wait_recv()
                pass_on(k, row, j).start()

        action(r)
        others(action)

    def stage5(k):
        others(lambda to: exchange(k, to).wait_send())
        for row in range(rows):
            gather(k, row, 0).wait()
            gather(k, row, chips).wait_recv()
            for j in range(1, chips):
                pass_on(k, row, j).wait()
            for j in range(1, chips + 1):
                gather(k, row, j).wait_send()

    def w_copy(g, part):
        return pltpu.make_async_copy(
            weight.at[part, :, :, aligned(g, width)], b["wv"].at[g, :, part], b["w_sem"].at[g, part]
        )

    for k in range(pn.ahead):
        stage1(k)

    @pl.loop(0, slices)
    def _(g):
        for part in range(ratio):
            w_copy(g, part).start()

    stage2(0)
    gather_row(0, r, own=True)
    for k in range(1, pn.ahead):
        stage2(k)
    stage3(0, with_own=False)
    stage4(0)

    def place(v):
        return aligned(v // slices, size), aligned(v % slices, width)

    def up(v):
        k, g = v // slices, v % slices

        @pl.when(g == 0)
        def _():
            stage5(k)

        @pl.when(k == 0)
        def _():
            for part in range(ratio):
                w_copy(g, part).wait()

        b["part"][v % pn.hold] = jnp.dot(
            b["tok"][k].reshape(rows * size, pn.features),
            b["wv"][g].reshape(pn.features, width),
            preferred_element_type=jnp.float32,
        )

    def towards(way):
        return r if way == 0 else far - r

    def sum_copy(v, way, h):
        slot = v % OUT_SLOTS
        return remote(
            b["rout"].at[slot, way, h],
            b["rin"].at[v % pn.in_slots, way, h],
            b["rss"].at[slot, way, h],
            b["rsr"].at[v % pn.in_slots, way, h],
            ((r + 1) % rows if way == 0 else (r + far) % rows, c),
        )

    def sums(v, h):
        for way in (0, 1):
            pos = towards(way)

            @pl.when(pos <= h)
            def _(way=way, pos=pos):
                @pl.when(v >= OUT_SLOTS)
                def _():
                    sum_copy(v, way, h).wait_send()

                owner = pos + far - h
                owner = owner if way == 0 else far - owner
                mine = b["part"].at[v % pn.hold, aligned(owner, size), :]
                out = b["rout"].at[v % OUT_SLOTS, way, h]

                @pl.when(pos == 0)
                def _():
                    out[...] = mine[...].astype(jnp.bfloat16)

                if h:

                    @pl.when(pos > 0)
                    def _():
                        sum_copy(v, way, h - 1).wait_recv()
                        got = b["rin"][v % pn.in_slots, way, h - 1]
                        out[...] = (got.astype(jnp.float32) + mine[...]).astype(jnp.bfloat16)

                sum_copy(v, way, h).start()

    def og_copy(v):
        return pltpu.make_async_copy(out_grad.at[place(v)], b["og"].at[v % 2], b["og_sem"].at[v % 2])

    def pre_copy(v):
        return pltpu.make_async_copy(b["pre"].at[v % 2], preact.at[place(v)], b["pre_sem"].at[v % 2])

    def grad_copy(v, way, h):
        slot = v % pn.grad_slots
        source = lax.rem(r + (rows - h if way == 0 else h), rows)
        block = b["grad"].at[slot, source]
        return remote(
            block,
            block,
            b["ags"].at[slot, way, h],
            b["agr"].at[slot, way, h],
            ((r + 1) % rows if way == 0 else (r + far) % rows, c),
        )

    def slope(v):
        mine = b["part"].at[v % pn.hold, aligned(r, size), :]
        for way in (0, 1):

            @pl.when(towards(way) > 0)
            def _(way=way):
                sum_copy(v, way, far - 1).wait_recv()
                mine[...] += b["rin"][v % pn.in_slots, way, far - 1].astype(jnp.float32)

        og_copy(v).wait()

        @pl.when(v >= 2)
        def _():
            pre_copy(v).wait()

        full_pre = mine[...]
        gradient = b["og"][v % 2].astype(jnp.float32) * gelu_slope(full_pre)
        b["grad"][v % pn.grad_slots, r] = gradient.astype(jnp.bfloat16)
        for way in (0, 1):

            @pl.when(towards(way) < far)
            def _(way=way):
                grad_copy(v, way, 0).start()

        b["pre"][v % 2] = full_pre.astype(jnp.bfloat16)
        pre_copy(v).start()

        @pl.when(v + 1 < units)
        def _():
            og_copy(v + 1).start()

    def grads(v, h):
        for way in (0, 1):

            @pl.when(towards(way) >= h)
            def _(way=way):
                grad_copy(v, way, h - 1).wait_recv()

                @pl.when(towards(way) < far)
                def _():
                    grad_copy(v, way, h).start()

    def down(v):
        k, g = v // slices, v % slices
        for way in (0, 1):

            @pl.when(towards(way) == far)
            def _(way=way):
                grad_copy(v, way, far - 1).wait_recv()

        acc = b["acc"].at[k % 2]

        @pl.when(g == 0)
        def _():
            acc[...] = jnp.zeros_like(acc)

        group = max(1, min(512 // piece, across))
        blocks = b["grad"][v % pn.grad_slots].reshape(rows * size, width)
        for n in range(0, across, group):
            part = lax.dot_general(
                blocks,
                b["wv"][g, n : n + group].reshape(group * piece, width),
                (((1,), (1,)), ((), ())),
                preferred_element_type=jnp.float32,
            )
            for m in range(group):
                acc[n + m] += part[:, m * piece : (m + 1) * piece].reshape(rows, size, piece)
        for way in (0, 1):
            for h in range(far):

                @pl.when((towards(way) >= h) & (towards(way) < far))
                def _(way=way, h=h):
                    grad_copy(v, way, h).wait_send()

    def pair_copy(k, j):
        return remote(
            b["x_out"].at[j], b["x_in"].at[k % 2, j], b["d1s"].at[j], b["d1r"].at[k % 2, j], (r, partner)
        )

    def plane_copy(k, j, row):
        to = ((chip + j) % chips) * 2 + core
        return remote(
            b["y_out"].at[j, row],
            b["y_in"].at[k % 2, j, row],
            b["d2s"].at[j, row],
            b["d2r"].at[k % 2, j, row],
            (r, to),
        )

    def row_copy(k, to):
        return remote(
            b["t_out"].at[to], b["t_in"].at[k % 2, r], b["d3s"].at[to], b["d3r"].at[k % 2, r], (to, c)
        )

    def row_arrival(k, source):
        return remote(
            b["t_out"].at[r], b["t_in"].at[k % 2, source], b["d3s"].at[r], b["d3r"].at[k % 2, source], (source, c)
        )

    def owned(k, q):
        down_part, side = tall(q)
        return input_grad.at[aligned(k * deep + down_part, short), aligned(side, thin)]

    def acc_part(k, q, row=None):
        down_part, side = tall(q)
        rows_of = slice(None) if row is None else row
        return b["acc"][k % 2, side, rows_of, aligned(down_part, short)]

    def owner_copy(k, to, local=False):
        src = b["t_in"].at[k % 2, to // ratio, :, aligned(to % ratio, thin)]
        dst = owned(k, c)
        if local:
            return pltpu.make_async_copy(src, dst, b["d4s"].at[c])
        return remote(src, dst, b["d4s"].at[to], b["d4r"].at[k, c], (r, to))

    def owner_arrival(k, source):
        src = b["t_in"].at[0, 0, :, aligned(0, thin)]
        dst = owned(k, source)
        return remote(src, dst, b["d4s"].at[source], b["d4r"].at[k, source], (r, source))

    def pair(k):
        for j in list(range(1, chips)) + [0]:

            @pl.when(k > 0)
            def _(j=j):
                pair_copy(k, j).wait_send()

            q = (chip + j) % chips
            b["x_out"][j] = acc_part(k, q * 2 + 1 - core).astype(jnp.bfloat16)
            pair_copy(k, j).start()

    def plane(k):
        for j in range(chips):
            pair_copy(k, j).wait_recv()

        def action(row):
            for j in range(1, chips):
                q = (chip + j) % chips

                @pl.when(k > 0)
                def _(j=j):
                    plane_copy(k, j, row).wait_send()

                total = acc_part(k, q * 2 + core, row) + b["x_in"][k % 2, j, row].astype(jnp.float32)
                b["y_out"][j, row] = total.astype(jnp.bfloat16)
                plane_copy(k, j, row).start()

        others(action, far_first=True)
        action(r)

    def owners_wait():
        for j in range(1, cols):
            owner_copy(0, (c + j) % cols).wait_send()
        owner_copy(0, c, local=True).wait()

    def exchange_back(k):
        @pl.when(k > 0)
        def _():
            owners_wait()
            others(lambda to: row_copy(k, to).wait_send())

        def total(row):
            value = acc_part(k, c, row) + b["x_in"][k % 2, 0, row].astype(jnp.float32)
            for j in range(1, chips):
                plane_copy(k, j, row).wait_recv()
                value = value + b["y_in"][k % 2, j, row].astype(jnp.float32)
            return value.astype(jnp.bfloat16)

        def action(row):
            b["t_out"][row] = total(row)
            row_copy(k, row).start()

        others(action, far_first=True)
        b["t_in"][k % 2, r] = total(r)

    def owners(k):
        def action(row):
            for part in range(ratio):
                to = row * ratio + part

                @pl.when(to != c)
                def _(to=to):
                    owner_copy(k, to).start()

                @pl.when(to == c)
                def _():
                    owner_copy(k, c, local=True).start()

        def arrived(row):
            row_arrival(k, row).wait_recv()
            action(row)

        action(r)
        others(arrived)

    def in_range(v):
        return (v >= 0) & (v < units)

    def at_chunk_end(v, action):
        @pl.when(in_range(v) & (v % slices == slices - 1))
        def _():
            action(v // slices)

    og_copy(0).start()
    ends = (0, 1, slices // 3, 2 * slices // 3)

    @pl.loop(0, units + pn.down_lag + ends[-1] + 1)
    def _(i):
        @pl.when(i < units)
        def _():
            up(i)

        for h in range(far):
            v = i - h * pn.lag

            @pl.when(in_range(v))
            def _(v=v, h=h):
                sums(v, h)

        @pl.when(in_range(i - pn.slope_lag))
        def _():
            slope(i - pn.slope_lag)

        for h in range(1, far):
            v = i - pn.slope_lag - h * pn.lag

            @pl.when(in_range(v))
            def _(v=v, h=h):
                grads(v, h)

        @pl.when(in_range(i - pn.down_lag))
        def _():
            down(i - pn.down_lag)

        for lag, action in zip(ends, (pair, plane, exchange_back, owners)):
            at_chunk_end(i - pn.down_lag - lag, action)

        for at, (action, early) in enumerate(
            ((stage1, pn.ahead), (stage2, pn.ahead), (stage3, 1), (stage4, 1))
        ):

            @pl.when((i < units - early * slices) & (i % slices == at * slices // 4))
            def _(action=action, early=early):
                action(i // slices + early)

    for back in range(1, OUT_SLOTS + 1):
        for way in (0, 1):
            for h in range(far):

                @pl.when(towards(way) <= h)
                def _(back=back, way=way, h=h):
                    sum_copy(units - back, way, h).wait_send()

    for v in (units - 2, units - 1):
        pre_copy(v).wait()
    last = pn.chunks - 1
    for j in range(chips):
        pair_copy(last, j).wait_send()
    for j in range(1, chips):
        for row in range(rows):
            plane_copy(last, j, row).wait_send()
    others(lambda to: row_copy(last, to).wait_send())
    owners_wait()

    @pl.loop(0, pn.chunks)
    def _(k):
        for j in range(1, cols):
            owner_arrival(k, (c + j) % cols).wait_recv()


def per_device(rows, cols, tokens, weight, out_grad):
    pn = Plan(rows, cols, tokens, weight)
    scratch = pn.scratch()
    anywhere = pl.BlockSpec(memory_space=pl.ANY)
    flops = 4 * pn.count * rows * pn.features * pn.hidden
    return pl.pallas_call(
        functools.partial(body, pn, tuple(scratch)),
        out_shape=(
            jax.ShapeDtypeStruct(out_grad.shape, jnp.bfloat16),
            jax.ShapeDtypeStruct(tokens.shape, jnp.bfloat16),
        ),
        in_specs=[anywhere] * 3,
        out_specs=(anywhere, anywhere),
        scratch_shapes=list(scratch.values()),
        compiler_params=pltpu.CompilerParams(
            collective_id=0, has_side_effects=True, vmem_limit_bytes=62 * 2**20
        ),
        cost_estimate=pl.CostEstimate(flops=flops, bytes_accessed=2 * weight.size, transcendentals=0),
    )(tokens, weight.reshape(pn.ratio, pn.across, pn.thin, pn.hidden), out_grad)


def solution(mesh):
    rows, cols = mesh.shape["row"], mesh.shape["col"]
    return jax.shard_map(
        functools.partial(per_device, rows, cols),
        mesh=mesh,
        in_specs=(P("row", "col"), P("row", "col"), P("row", "col")),
        out_specs=(P("row", "col"), P("row", "col")),
        check_vma=False,
    )
```

```python
import functools
import math

import jax
import jax.numpy as jnp
from jax import lax
from jax.experimental import pallas as pl
from jax.experimental.pallas import tpu as pltpu
from jax.sharding import PartitionSpec as P

sqrt_half = 1.0 / math.sqrt(2.0)
inv_root_tau = 1.0 / math.sqrt(2.0 * math.pi)

MESH = pl.DeviceIdType.MESH
CHUNKS = 8
WIDTH = 256
LAGS = 3, 2
OUT_SLOTS = 3
AHEAD = 6
REST_AT = 2
HELD = 5


def gelu_slope(values):
    return (
        0.5 * (1.0 + lax.erf(values * sqrt_half))
        + values * jnp.exp(-0.5 * values * values) * inv_root_tau
    )


class Plan:
    def __init__(self, rows, cols, tokens, weight):
        self.rows, self.cols = rows, cols
        self.count, self.share = tokens.shape
        self.features, self.hidden = weight.shape
        self.ratio = self.features // self.share
        self.chips = cols // 2
        self.chunks = CHUNKS
        self.size = self.count // CHUNKS
        self.thin = max(self.share // cols, min(self.share, 128))
        self.across = self.share // self.thin
        self.deep = cols // self.across
        self.short = self.size // self.deep
        self.piece = self.ratio * self.thin
        self.width = WIDTH if self.hidden % WIDTH == 0 else 128
        self.slices = self.hidden // self.width
        assert self.deep * self.short * CHUNKS == self.count and self.slices * self.width == self.hidden
        self.units = self.chunks * self.slices
        self.far = rows - 1
        self.ahead = min(AHEAD, self.chunks)
        lags = [m * LAGS[0] // LAGS[1] for m in range(2 * self.far + 1)]
        self.lags = lags
        self.slope_lag = lags[self.far]
        self.down_lag = lags[-1]
        self.hold = self.slope_lag + 1
        self.in_slots = self.slope_lag + 6
        self.grad_slots = self.down_lag - self.slope_lag + 6

    def scratch(self):
        bf, f4 = jnp.bfloat16, jnp.float32
        r, c, n, s, d = self.rows, self.cols, self.chunks, self.size, self.features
        far, w, piece, chips = self.far, self.width, self.piece, self.chips
        low = self.short
        dma = pltpu.SemaphoreType.DMA
        return dict(
            a1=pltpu.VMEM((n, r, low, piece), bf),
            a2=pltpu.VMEM((n, r, low, piece), bf),
            tok=pltpu.VMEM((n, r, s, d), bf),
            wv=pltpu.VMEM((self.slices, self.across, self.ratio, self.thin, w), bf),
            part=pltpu.VMEM((self.hold, r * s, w), f4),
            rin=pltpu.VMEM((self.in_slots, 2, far, s, w), bf),
            rout=pltpu.VMEM((OUT_SLOTS, 2, far, s, w), bf),
            grad=pltpu.VMEM((self.grad_slots, r, s, w), bf),
            og=pltpu.VMEM((2, s, w), bf),
            pre=pltpu.VMEM((2, s, w), bf),
            acc=pltpu.VMEM((2, self.across, r, s, piece), f4),
            x_out=pltpu.VMEM((chips, r, low, piece), bf),
            x_in=pltpu.VMEM((2, chips, r, low, piece), bf),
            y_out=pltpu.VMEM((chips, r, low, piece), bf),
            y_in=pltpu.VMEM((2, chips, r, low, piece), bf),
            t_out=pltpu.VMEM((n, r, low, piece), bf),
            t_in=pltpu.VMEM((n, r, low, piece), bf),
            w_sem=dma((self.slices, self.ratio)),
            s1s=dma((n, c)),
            s1r=dma((n, c)),
            s2s=dma((n, r)),
            s2r=dma((n, r)),
            s3s=dma((2, r, chips + 1)),
            s3r=dma((2, r, chips + 1)),
            s4s=dma((2, r, chips)),
            s4r=dma((2, r, chips)),
            rss=dma((OUT_SLOTS, 2, far)),
            rsr=dma((self.in_slots, 2, far)),
            ags=dma((self.grad_slots, 2, far)),
            agr=dma((self.grad_slots, 2, far)),
            og_sem=dma((2,)),
            pre_sem=dma((2,)),
            d1s=dma((chips,)),
            d1r=dma((2, chips)),
            d2s=dma((chips, r)),
            d2r=dma((2, chips, r)),
            d3s=dma((n, r)),
            d3r=dma((n, r)),
            d4s=dma((n, c)),
            d4r=dma((n, c)),
        )


def aligned(index, size):
    return pl.ds(pl.multiple_of(index * size, size), size)


def body(pn, names, tokens, weight, out_grad, preact, input_grad, *refs):
    b = dict(zip(names, refs))
    rows, cols, chips, far = pn.rows, pn.cols, pn.chips, pn.far
    size, piece, width, thin = pn.size, pn.piece, pn.width, pn.thin
    units, slices, ratio = pn.units, pn.slices, pn.ratio
    r, c = lax.axis_index("row"), lax.axis_index("col")
    core, chip = c % 2, c // 2
    partner = c + 1 - 2 * core
    across, deep, short = pn.across, pn.deep, pn.short

    def tall(q):
        return (q // across if deep > 1 else 0), (q % across if deep > 1 else q)


    def remote(src, dst, send, recv, to):
        return pltpu.make_async_remote_copy(
            src_ref=src, dst_ref=dst, send_sem=send, recv_sem=recv, device_id=to, device_id_type=MESH
        )

    barrier = pltpu.get_barrier_semaphore()
    for j in range(1, rows):
        pl.semaphore_signal(barrier, inc=1, device_id=((r + j) % rows, c), device_id_type=MESH)
    for j in range(1, cols):
        pl.semaphore_signal(barrier, inc=1, device_id=(r, (c + j) % cols), device_id_type=MESH)
    pl.semaphore_wait(barrier, rows + cols - 2)

    def others(action, far_first=False):
        steps = [s for d in range(1, rows) for s in (d, -d)]
        for s in steps[::-1] if far_first else steps:

            @pl.when((r + s >= 0) & (r + s < rows))
            def _(s=s):
                action(r + s)

    def spread(k, j):
        to = (c + j) % cols
        down_part, side = tall(to)
        src = tokens.at[aligned(k * deep + down_part, short), aligned(side, thin)]
        dst = b["a1"].at[k, c // ratio, :, aligned(c % ratio, thin)]
        if not j:
            return pltpu.make_async_copy(src, dst, b["s1s"].at[k, 0])
        return remote(src, dst, b["s1s"].at[k, j], b["s1r"].at[k, j], (r, to))

    def exchange(k, to):
        return remote(
            b["a1"].at[k, to], b["a2"].at[k, r], b["s2s"].at[k, to], b["s2r"].at[k, r], (to, c)
        )

    def exchanged(k, source):
        return remote(
            b["a1"].at[k, r], b["a2"].at[k, source], b["s2s"].at[k, r], b["s2r"].at[k, source], (source, c)
        )

    def token_part(k, row, q):
        down_part, side = tall(q)
        return b["tok"].at[k, row, aligned(down_part, short), aligned(side, piece)]

    def gather(k, row, j, own=False):
        src = b["a1"].at[k, r] if own else b["a2"].at[k, row]
        dst = token_part(k, row, c)
        send = b["s3s"].at[k % 2, row, j]
        if not j:
            return pltpu.make_async_copy(src, dst, send)
        to = partner if j == chips else ((chip + j) % chips) * 2 + core
        return remote(src, dst, send, b["s3r"].at[k % 2, row, j], (r, to))

    def pass_on(k, row, j):
        here = token_part(k, row, ((chip - j + chips) % chips) * 2 + core)
        return remote(here, here, b["s4s"].at[k % 2, row, j], b["s4r"].at[k % 2, row, j], (r, partner))

    def stage1(k):
        for j in range(1, cols):
            spread(k, j).start()
        spread(k, 0).start()

    def stage2(k):
        spread(k, 0).wait()
        for j in range(1, cols):
            spread(k, j).wait_recv()
        others(lambda to: exchange(k, to).start(), far_first=True)
        for j in range(1, cols):
            spread(k, j).wait_send()

    def gather_row(k, row, own=False):
        for j in list(range(1, chips + 1)) + [0]:
            gather(k, row, j, own).start()

    def stage3(k, with_own=True):
        if with_own:
            gather_row(k, r, own=True)

        def action(row):
            exchanged(k, row).wait_recv()
            gather_row(k, row)

        others(action)

    def stage4(k):
        def action(row):
            for j in range(1, chips):
                gather(k, row, j).wait_recv()
                pass_on(k, row, j).start()

        action(r)
        others(action)

    def stage5(k):
        others(lambda to: exchange(k, to).wait_send())
        for row in range(rows):
            gather(k, row, 0).wait()
            gather(k, row, chips).wait_recv()
            for j in range(1, chips):
                pass_on(k, row, j).wait()
            for j in range(1, chips + 1):
                gather(k, row, j).wait_send()

    def w_copy(g, part):
        return pltpu.make_async_copy(
            weight.at[part, :, :, aligned(g, width)], b["wv"].at[g, :, part], b["w_sem"].at[g, part]
        )

    for k in range(pn.ahead):
        stage1(k)

    @pl.loop(0, slices)
    def _(g):
        for part in range(ratio):
            w_copy(g, part).start()

    stage2(0)
    gather_row(0, r, own=True)
    for k in range(1, pn.ahead):
        stage2(k)
    stage3(0, with_own=False)
    stage4(0)
    for k in range(pn.ahead, pn.chunks):
        stage1(k)

    def place(v):
        return aligned(v // slices, size), aligned(v % slices, width)

    def up(v):
        k, g = v // slices, v % slices

        @pl.when(g == 0)
        def _():
            stage5(k)

        @pl.when(k == 0)
        def _():
            for part in range(ratio):
                w_copy(g, part).wait()

        b["part"][v % pn.hold] = jnp.dot(
            b["tok"][k].reshape(rows * size, pn.features),
            b["wv"][g].reshape(pn.features, width),
            preferred_element_type=jnp.float32,
        )

    def towards(way):
        return r if way == 0 else far - r

    def sum_copy(v, way, h):
        slot = v % OUT_SLOTS
        return remote(
            b["rout"].at[slot, way, h],
            b["rin"].at[v % pn.in_slots, way, h],
            b["rss"].at[slot, way, h],
            b["rsr"].at[v % pn.in_slots, way, h],
            ((r + 1) % rows if way == 0 else (r + far) % rows, c),
        )

    def sums(v, h):
        for way in (0, 1):
            pos = towards(way)

            @pl.when(pos <= h)
            def _(way=way, pos=pos):
                @pl.when(v >= OUT_SLOTS)
                def _():
                    sum_copy(v, way, h).wait_send()

                owner = pos + far - h
                owner = owner if way == 0 else far - owner
                mine = b["part"].at[v % pn.hold, aligned(owner, size), :]
                out = b["rout"].at[v % OUT_SLOTS, way, h]

                @pl.when(pos == 0)
                def _():
                    out[...] = mine[...].astype(jnp.bfloat16)

                if h:

                    @pl.when(pos > 0)
                    def _():
                        sum_copy(v, way, h - 1).wait_recv()
                        got = b["rin"][v % pn.in_slots, way, h - 1]
                        out[...] = (got.astype(jnp.float32) + mine[...]).astype(jnp.bfloat16)

                sum_copy(v, way, h).start()

    def og_copy(v):
        return pltpu.make_async_copy(out_grad.at[place(v)], b["og"].at[v % 2], b["og_sem"].at[v % 2])

    def pre_copy(v):
        return pltpu.make_async_copy(b["pre"].at[v % 2], preact.at[place(v)], b["pre_sem"].at[v % 2])

    def grad_copy(v, way, h):
        slot = v % pn.grad_slots
        source = lax.rem(r + (rows - h if way == 0 else h), rows)
        block = b["grad"].at[slot, source]
        return remote(
            block,
            block,
            b["ags"].at[slot, way, h],
            b["agr"].at[slot, way, h],
            ((r + 1) % rows if way == 0 else (r + far) % rows, c),
        )

    def slope(v):
        mine = b["part"].at[v % pn.hold, aligned(r, size), :]
        for way in (0, 1):

            @pl.when(towards(way) > 0)
            def _(way=way):
                sum_copy(v, way, far - 1).wait_recv()
                mine[...] += b["rin"][v % pn.in_slots, way, far - 1].astype(jnp.float32)

        og_copy(v).wait()

        @pl.when(v >= 2)
        def _():
            pre_copy(v).wait()

        full_pre = mine[...]
        gradient = b["og"][v % 2].astype(jnp.float32) * gelu_slope(full_pre)
        b["grad"][v % pn.grad_slots, r] = gradient.astype(jnp.bfloat16)
        for way in (0, 1):

            @pl.when(towards(way) < far)
            def _(way=way):
                grad_copy(v, way, 0).start()

        b["pre"][v % 2] = full_pre.astype(jnp.bfloat16)
        pre_copy(v).start()

        @pl.when(v + 1 < units)
        def _():
            og_copy(v + 1).start()

    def grads(v, h):
        for way in (0, 1):

            @pl.when(towards(way) >= h)
            def _(way=way):
                grad_copy(v, way, h - 1).wait_recv()

                @pl.when(towards(way) < far)
                def _():
                    grad_copy(v, way, h).start()

    def down(v):
        k, g = v // slices, v % slices
        for way in (0, 1):

            @pl.when(towards(way) == far)
            def _(way=way):
                grad_copy(v, way, far - 1).wait_recv()

        acc = b["acc"].at[k % 2]

        @pl.when(g == 0)
        def _():
            acc[...] = jnp.zeros_like(acc)

        group = max(1, min(512 // piece, across))
        blocks = b["grad"][v % pn.grad_slots].reshape(rows * size, width)
        for n in range(0, across, group):
            part = lax.dot_general(
                blocks,
                b["wv"][g, n : n + group].reshape(group * piece, width),
                (((1,), (1,)), ((), ())),
                preferred_element_type=jnp.float32,
            )
            for m in range(group):
                acc[n + m] += part[:, m * piece : (m + 1) * piece].reshape(rows, size, piece)
        for way in (0, 1):
            for h in range(far):

                @pl.when((towards(way) >= h) & (towards(way) < far))
                def _(way=way, h=h):
                    grad_copy(v, way, h).wait_send()

    def pair_copy(k, j):
        return remote(
            b["x_out"].at[j], b["x_in"].at[k % 2, j], b["d1s"].at[j], b["d1r"].at[k % 2, j], (r, partner)
        )

    def plane_copy(k, j, row):
        to = ((chip + j) % chips) * 2 + core
        return remote(
            b["y_out"].at[j, row],
            b["y_in"].at[k % 2, j, row],
            b["d2s"].at[j, row],
            b["d2r"].at[k % 2, j, row],
            (r, to),
        )

    def row_copy(k, to):
        return remote(
            b["t_out"].at[k, to], b["t_in"].at[k, r], b["d3s"].at[k, to], b["d3r"].at[k, r], (to, c)
        )

    def row_arrival(k, source):
        return remote(
            b["t_out"].at[k, r], b["t_in"].at[k, source], b["d3s"].at[k, r], b["d3r"].at[k, source], (source, c)
        )

    def owned(k, q):
        down_part, side = tall(q)
        return input_grad.at[aligned(k * deep + down_part, short), aligned(side, thin)]

    def acc_part(k, q, row=None):
        down_part, side = tall(q)
        rows_of = slice(None) if row is None else row
        return b["acc"][k % 2, side, rows_of, aligned(down_part, short)]

    def owner_copy(k, to, local=False):
        src = b["t_in"].at[k, to // ratio, :, aligned(to % ratio, thin)]
        dst = owned(k, c)
        if local:
            return pltpu.make_async_copy(src, dst, b["d4s"].at[k, c])
        return remote(src, dst, b["d4s"].at[k, to], b["d4r"].at[k, c], (r, to))

    def owner_arrival(k, source):
        src = b["t_in"].at[0, 0, :, aligned(0, thin)]
        dst = owned(k, source)
        return remote(src, dst, b["d4s"].at[k, source], b["d4r"].at[k, source], (r, source))

    def pair(k):
        for j in list(range(1, chips)) + [0]:

            @pl.when(k > 0)
            def _(j=j):
                pair_copy(k, j).wait_send()

            q = (chip + j) % chips
            b["x_out"][j] = acc_part(k, q * 2 + 1 - core).astype(jnp.bfloat16)
            pair_copy(k, j).start()

    def plane(k):
        for j in range(chips):
            pair_copy(k, j).wait_recv()

        def action(row):
            for j in range(1, chips):
                q = (chip + j) % chips

                @pl.when(k > 0)
                def _(j=j):
                    plane_copy(k, j, row).wait_send()

                total = acc_part(k, q * 2 + core, row) + b["x_in"][k % 2, j, row].astype(jnp.float32)
                b["y_out"][j, row] = total.astype(jnp.bfloat16)
                plane_copy(k, j, row).start()

        others(action, far_first=True)
        action(r)

    def exchange_back(k):
        def total(row):
            value = acc_part(k, c, row) + b["x_in"][k % 2, 0, row].astype(jnp.float32)
            for j in range(1, chips):
                plane_copy(k, j, row).wait_recv()
                value = value + b["y_in"][k % 2, j, row].astype(jnp.float32)
            return value.astype(jnp.bfloat16)

        send = (k < pn.chunks - HELD) | (k == pn.chunks - 1)

        def action(row):
            b["t_out"][k, row] = total(row)
            pl.when(send)(lambda: row_copy(k, row).start())

        others(action, far_first=True)
        b["t_in"][k, r] = total(r)

    def send_held():
        for k in range(max(pn.chunks - HELD, 0), pn.chunks - 1):
            others(lambda to: row_copy(k, to).start(), far_first=True)

    def owners(k):
        def action(row):
            for part in range(ratio):
                to = row * ratio + part

                @pl.when(to != c)
                def _(to=to):
                    owner_copy(k, to).start()

                @pl.when(to == c)
                def _():
                    owner_copy(k, c, local=True).start()

        def arrived(row):
            row_arrival(k, row).wait_recv()
            action(row)

        action(r)
        others(arrived)

    def in_range(v):
        return (v >= 0) & (v < units)

    def at_chunk_end(v, action):
        @pl.when(in_range(v) & (v % slices == slices - 1))
        def _():
            action(v // slices)

    og_copy(0).start()
    ends = (0, 1, slices // 3, 2 * slices // 3)
    freed = units + pn.lags[2 * far - 1]

    @pl.loop(0, units + pn.down_lag + ends[2] + 1)
    def _(i):
        def step(m):
            v = i - pn.lags[m]

            @pl.when(in_range(v))
            def _():
                if m < far:
                    sums(v, m)
                elif m == far:
                    slope(v)
                elif m < 2 * far:
                    grads(v, m - far)
                else:
                    down(v)

        @pl.when(i < units)
        def _():
            up(i)

        for half in (0, 1):
            for m in range(half, 2 * far + 1, 2):
                step(m)

        pl.when(i == freed)(send_held)

        def early_owners(k):
            pl.when(k < pn.chunks - HELD)(lambda: owners(k))

        for lag, action in zip(ends, (pair, plane, exchange_back, early_owners)):
            at_chunk_end(i - pn.down_lag - lag, action)

        rest = i - REST_AT

        @pl.when((rest >= 0) & (rest < pn.chunks - pn.ahead))
        def _():
            stage2(rest + pn.ahead)

        for at, action in ((2, stage3), (3, stage4)):

            @pl.when((i < units - slices) & (i % slices == at * slices // 4))
            def _(action=action):
                action(i // slices + 1)

    for back in range(1, OUT_SLOTS + 1):
        for way in (0, 1):
            for h in range(far):

                @pl.when(towards(way) <= h)
                def _(back=back, way=way, h=h):
                    sum_copy(units - back, way, h).wait_send()

    @pl.loop(max(pn.chunks - HELD, 0), pn.chunks)
    def _(k):
        owners(k)

    for v in (units - 2, units - 1):
        pre_copy(v).wait()
    last = pn.chunks - 1
    for j in range(chips):
        pair_copy(last, j).wait_send()
    for j in range(1, chips):
        for row in range(rows):
            plane_copy(last, j, row).wait_send()

    @pl.loop(0, pn.chunks)
    def _(k):
        others(lambda to: row_copy(k, to).wait_send())
        owner_copy(k, c, local=True).wait()
        for j in range(1, cols):
            owner_arrival(k, (c + j) % cols).wait_recv()
            owner_copy(k, (c + j) % cols).wait_send()


def per_device(rows, cols, tokens, weight, out_grad):
    pn = Plan(rows, cols, tokens, weight)
    scratch = pn.scratch()
    anywhere = pl.BlockSpec(memory_space=pl.ANY)
    flops = 4 * pn.count * rows * pn.features * pn.hidden
    return pl.pallas_call(
        functools.partial(body, pn, tuple(scratch)),
        out_shape=(
            jax.ShapeDtypeStruct(out_grad.shape, jnp.bfloat16),
            jax.ShapeDtypeStruct(tokens.shape, jnp.bfloat16),
        ),
        in_specs=[anywhere] * 3,
        out_specs=(anywhere, anywhere),
        scratch_shapes=list(scratch.values()),
        compiler_params=pltpu.CompilerParams(
            collective_id=0, has_side_effects=True, vmem_limit_bytes=62 * 2**20
        ),
        cost_estimate=pl.CostEstimate(flops=flops, bytes_accessed=2 * weight.size, transcendentals=0),
    )(tokens, weight.reshape(pn.ratio, pn.across, pn.thin, pn.hidden), out_grad)


def solution(mesh):
    rows, cols = mesh.shape["row"], mesh.shape["col"]
    return jax.shard_map(
        functools.partial(per_device, rows, cols),
        mesh=mesh,
        in_specs=(P("row", "col"), P("row", "col"), P("row", "col")),
        out_specs=(P("row", "col"), P("row", "col")),
        check_vma=False,
    )
```
